256 devices in a mesh: seg: 32 (over z, y), op: 8 (over x, core).
Axes of the slice: x: 4, y: 4, z: 8, core: 2. Of those that a mesh axis runs over, the one named last changes fastest.
Arguments:
- label_map: int32 [32, 16], P('seg'), may hold values from 0 to 15, each once within a row
- site_blocks: float32 [32, 16, 128, 128], P('seg'), may hold values from -0.25 to 1.25
- left_ops: bfloat16 [96, 16, 128, 128], P('op'), may hold values from -0.5 to 0.5
- right_ops: bfloat16 [32, 96, 16, 128, 128], P('seg', 'op'), may hold values from -0.0546875 to 0.0546875
- wavefunction: bfloat16 [32, 16, 128, 128], P('seg', 'op'), may hold values from -72 to 72
Outputs:
- ham_psi: bfloat16 [32, 16, 128, 128], P('seg', 'op')
- ham_squared_psi: bfloat16 [32, 16, 128, 128], P('seg', 'op')
The draws below stay inside these ranges and needn't reach their ends.
Inputs may be any that keep to these rules, and one draw needn't show every extreme that they name: Each row of label_map is a permutation of 0 to 15.
All inputs are finite; a program needn't handle non-finite values.
Results may differ from the reference program's by a relative error of at most 0.022.
Values may be sent and summed in bfloat16 or wider, within the bound.
No kernel may reach another device: no remote copies, remote signals or barrier semaphores. Data moves between devices by JAX's collectives and lax.ppermute only.
A program may use at most 128 MiB of HBM per device.

```python
import math
import jax
import jax.numpy as jnp
from jax import lax

NB = 16
BS = 128
OPS = 96
NSEG = 32


def draw_site_blocks(key, part):
    array_shape = (NSEG, NB, BS, BS)
    fluctuation = jnp.clip(jax.random.normal(key, array_shape, jnp.float32), -4.0, 4.0)
    unit_diagonal = (jnp.arange(BS)[:, None] == jnp.arange(BS)[None, :]).astype(jnp.float32)
    return (unit_diagonal + 0.25 * fluctuation / math.sqrt(BS)) / math.sqrt(1.0625)


def draw_wavefunction(key, part):
    key_list = jax.random.split(key, 4)
    array_shape = (NSEG, NB, BS, BS)
    base_vals = jnp.clip(jax.random.normal(key_list[0], array_shape, jnp.float32), -4.0, 4.0)
    row_scale = jnp.exp(jax.random.uniform(key_list[1], (NSEG, NB, BS, 1), jnp.float32, math.log(0.4), math.log(4.0)))
    col_scale = jnp.exp(jax.random.uniform(key_list[2], (NSEG, NB, 1, BS), jnp.float32, math.log(0.4), math.log(4.0)))
    rising = jnp.power(3.0, jnp.arange(NB, dtype=jnp.float32) / max(NB - 1, 1))[None, :, None, None]
    jitter = jax.random.uniform(key_list[3], (NSEG, NB, 1, 1), jnp.float32, 0.8, 1.25)
    return (0.3 * base_vals * row_scale * col_scale * rising * jitter).astype(jnp.bfloat16)


def shard_levels(key, dims, shards, least, largest):
    level = 1.0
    for axis_at, parts in shards:
        heights = jax.random.uniform(jax.random.fold_in(jax.random.fold_in(key, 6), axis_at), (parts,), jnp.float32, least / len(shards), largest / len(shards))
        level = level * jnp.repeat(jnp.exp(heights), dims[axis_at] // parts).reshape((-1,) + (1,) * (len(dims) - 1 - axis_at))
    return level


def scatter_about(key, dims, deviation, bound, cuts=(), held_as=jnp.bfloat16):
    values = deviation * jax.random.normal(key, dims, jnp.float32)
    if cuts:
        values = values * shard_levels(key, dims, cuts, -0.22, 0.18)
    return jnp.clip(values, -bound, bound).astype(held_as)


def setup_inputs(seed: int = 0) -> dict:
    key_of = jax.random.split(jax.random.key(seed), 6)
    label_map = jax.vmap(lambda own: jax.random.permutation(own, NB))(jax.random.split(key_of[0], NSEG)).reshape((NSEG, NB)).astype(jnp.int32)
    site_blocks = draw_site_blocks(jax.random.fold_in(key_of[5], 71), 0)
    left_ops = scatter_about(key_of[2], (OPS, NB, BS, BS), BS ** -0.5, 0.5, ((0, 8),))
    right_ops = scatter_about(key_of[3], (NSEG, OPS, NB, BS, BS), (BS * OPS) ** -0.5, 0.0546875, ((0, 32), (1, 8)))
    wavefunction = draw_wavefunction(jax.random.fold_in(key_of[5], 71), 0)
    return {"label_map": label_map, "site_blocks": site_blocks, "left_ops": left_ops, "right_ops": right_ops, "wavefunction": wavefunction}


def reference(label_map, site_blocks, left_ops, right_ops, wavefunction):
    highest = lax.Precision.HIGHEST
    identity = jnp.eye(BS, dtype=jnp.float32)

    def advance(state_pair, inputs):
        blocks, labels = state_pair
        site_seg, map_seg = inputs
        picked = jnp.take(site_seg, labels, axis=0)
        new_blocks = jnp.einsum('qij,qjk->qik', blocks, picked, precision=highest)
        new_labels = jnp.take(map_seg, labels).astype(jnp.int32)
        return ((new_blocks, new_labels), (blocks, labels))
    initial = (jnp.broadcast_to(identity, (NB, BS, BS)).astype(jnp.float32), jnp.arange(NB, dtype=jnp.int32))
    final_state, (prefix, labels) = lax.scan(advance, initial, (site_blocks, label_map.astype(jnp.int32)))
    left_wide = left_ops.astype(jnp.float32)

    def segment(inputs):
        seg_prefix, seg_labels, seg_right, seg_psi = inputs
        inverse = jnp.argsort(seg_labels).astype(jnp.int32)
        inner_prod = jnp.einsum('kqjl,qlm->kqjm', left_wide, seg_prefix, precision=highest)
        environ = jnp.einsum('qji,kqjm->kqim', seg_prefix, inner_prod, precision=highest)
        environ = jnp.take(environ, inverse, axis=1).astype(jnp.bfloat16)
        env_wide = environ.astype(jnp.float32)
        right_wide = seg_right.astype(jnp.float32)

        def apply_ham(vector):
            half_prod = jnp.einsum('kpij,pjl->kpil', env_wide, vector.astype(jnp.float32)).astype(jnp.bfloat16)
            return jnp.einsum('kpil,kpml->pim', half_prod.astype(jnp.float32), right_wide)
        hpsi_sum = apply_ham(seg_psi)
        scale_fac = lax.rsqrt(jnp.sum(hpsi_sum * hpsi_sum) / (NB * BS * BS) + 1e-06)
        unit_vec = (hpsi_sum * scale_fac).astype(jnp.bfloat16)
        second = apply_ham(unit_vec).astype(jnp.bfloat16)
        return (hpsi_sum.astype(jnp.bfloat16), second)
    ham_psi, ham_squared_psi = lax.map(segment, (prefix, labels, right_ops, wavefunction))
    return (ham_psi, ham_squared_psi)
```

```python
import functools

import jax
import jax.numpy as jnp
from jax import lax
from jax.experimental import pallas as pl
from jax.experimental.pallas import tpu as pltpu
from jax.sharding import Mesh
from jax.sharding import PartitionSpec as P

SEG = ("z", "y")
OP = ("x", "c")
NZ, NY, NX, NC = 8, 4, 4, 2
N = 128
CODE_ROWS = N + 16
SCALE = 2.0**-27
UNSCALE = 2.0**54
HIGHEST = lax.Precision.HIGHEST
VMEM = pl.BlockSpec(memory_space=pltpu.VMEM)
SMEM = pl.BlockSpec(memory_space=pltpu.SMEM)
LN2 = 0.6931471805599453


def shift(n, d):
    return [(i, (i + d) % n) for i in range(n)]


def call(kernel, outs, specs, out_specs, args, scratch=(), flops=0, limit=None):
    return pl.pallas_call(
        kernel,
        out_shape=outs,
        in_specs=specs,
        out_specs=out_specs,
        scratch_shapes=list(scratch),
        cost_estimate=pl.CostEstimate(flops=flops, bytes_accessed=1 << 20, transcendentals=0),
        compiler_params=pltpu.CompilerParams(vmem_limit_bytes=limit),
    )(*args)


def encode(x):
    top = jnp.maximum(jnp.max(jnp.abs(x), axis=0, keepdims=True), 1e-30)
    power = jnp.ceil(jnp.log(top) * (1.0 / LN2))
    coded = jnp.round(x * (jnp.exp(power * -LN2) * 32760.0)).astype(jnp.int32)
    powers = jnp.broadcast_to(power, (16, N)).astype(jnp.int32)
    return coded.astype(jnp.int16), powers.astype(jnp.int16)


def decode(ref):
    coded = ref[0:N, :].astype(jnp.int32).astype(jnp.float32)
    power = ref[N:CODE_ROWS, :].astype(jnp.int32).astype(jnp.float32)[0:1, :]
    return coded * (jnp.exp(power * LN2) * (1.0 / 32760.0))


def mm(a, b):
    return jnp.dot(a, b, precision=HIGHEST, preferred_element_type=jnp.float32)


def select_kernel(at_ref, maps_ref, blocks_ref, code_ref, inverse_ref):
    seg = at_ref[0]
    own = at_ref[1]

    def step(s, labels):
        return tuple(maps_ref[s, label] for label in labels)

    labels = lax.fori_loop(0, seg, step, tuple(jnp.int32(q) for q in range(16)))
    for q in range(16):
        inverse_ref[labels[q]] = jnp.int32(q)
    for i in range(2):
        label = jnp.int32(0)
        for q in range(16):
            label = jnp.where(own * 2 + i == q, labels[q], label)
        coded, powers = encode(blocks_ref[label])
        code_ref[i, 0:N, :] = coded
        code_ref[i, N:CODE_ROWS, :] = powers


def row_kernel(at_ref, s0, s1, s2, s3, code_ref, before_ref, held):
    y = at_ref[2]
    for d, ref in enumerate((s0, s1, s2, s3)):
        for i in range(2):
            held[lax.rem(y - d + NY, NY), i] = decode(ref.at[i])
    diagonal = lax.broadcasted_iota(jnp.int32, (N, N), 0) == lax.broadcasted_iota(
        jnp.int32, (N, N), 1
    )
    identity = diagonal.astype(jnp.float32)
    for i in range(2):
        first = mm(held[0, i], held[1, i])
        last = mm(held[2, i], held[3, i])
        three = mm(first, held[2, i])
        coded, powers = encode(mm(first, last))
        for z in range(NZ):
            code_ref[z, i, 0:N, :] = coded
            code_ref[z, i, N:CODE_ROWS, :] = powers
        low = jnp.where(y == 0, identity, held[0, i])
        high = jnp.where(y == 2, first, three)
        before_ref[i] = jnp.where(y < 2, low, high)


def chain_kernel(at_ref, codes_ref, before_ref, psi_ref, out_ref):
    z = at_ref[3]
    diagonal = lax.broadcasted_iota(jnp.int32, (N, N), 0) == lax.broadcasted_iota(
        jnp.int32, (N, N), 1
    )
    identity = diagonal.astype(jnp.float32)
    for i in range(2):
        factors = [
            jnp.where(k < z, decode(codes_ref.at[k, i]), identity) for k in range(NZ - 1)
        ] + [before_ref[i]]
        while len(factors) > 1:
            factors = [mm(factors[j], factors[j + 1]) for j in range(0, len(factors), 2)]
        out_ref[i] = (factors[0] * SCALE).astype(jnp.bfloat16)
        out_ref[2 + i] = psi_ref[i]


def sources(at_ref):
    own, x, c = at_ref[1], at_ref[4], at_ref[5]
    return [
        lax.rem(x - d + NX, NX) * 2 + (c if same == 0 else 1 - c)
        for d in range(NX)
        for same in range(2)
    ]


def apply_sector(k_ops, phi, left_ref, q, right_ref, p):
    rows = []
    for k in range(k_ops):
        rows.append(
            jnp.dot(left_ref[k, q], phi, preferred_element_type=jnp.float32).astype(jnp.bfloat16)
        )
    half = jnp.concatenate(rows, axis=1)
    right = jnp.concatenate([right_ref[k, p] for k in range(k_ops)], axis=1)
    return lax.dot_general(
        half, right, (((1,), (1,)), ((), ())), preferred_element_type=jnp.float32
    )


def apply_kernel(
    first, k_ops, at_ref, inverse_ref, left_ref, right_ref, *refs
):
    gathered = refs[:8]
    if first:
        keep_ref, send_ref, prefix_ref, prefixes, vectors = refs[8:]
    else:
        keep_ref, send_ref, total_ref, vectors = refs[8:]
    x, c = at_ref[4], at_ref[5]
    total = jnp.zeros((1, N), jnp.float32)
    for source, ref in zip(sources(at_ref), gathered):
        for i in range(2):
            if first:
                prefixes[source * 2 + i] = ref[i]
                vectors[source * 2 + i] = ref[2 + i]
            else:
                vectors[source * 2 + i] = ref[i * N : i * N + N, :]
        if not first:
            total += jnp.sum(ref[2 * N : 2 * N + 16, :].astype(jnp.float32), axis=0, keepdims=True)
    if first:
        for i in range(2):
            prefix_ref[i] = prefixes[inverse_ref[(x * 2 + c) * 2 + i]]
    else:
        total_ref[...] = jnp.broadcast_to(total, (8, N))

    for out_ref, core in ((send_ref, 1 - c), (keep_ref, c)):

        def body(j, carry, out_ref=out_ref, core=core):
            d = j // 2
            i = lax.rem(j, 2)
            p = (lax.rem(x + d, NX) * 2 + core) * 2 + i
            q = inverse_ref[p]
            if first:
                phi = jnp.dot(
                    prefixes[q], vectors[p], preferred_element_type=jnp.float32
                ).astype(jnp.bfloat16)
            else:
                phi = vectors[p]
            out_ref[d, i] = apply_sector(k_ops, phi, left_ref, q, right_ref, p).astype(
                jnp.bfloat16
            )
            return carry

        lax.fori_loop(0, 8, body, 0)


def add_kernel(keep_ref, other_ref, s0, s1, s2, s3):
    for d, ref in enumerate((s0, s1, s2, s3)):
        both = keep_ref[d].astype(jnp.float32) + other_ref[d].astype(jnp.float32)
        ref[...] = both.astype(ref.dtype)


def owner_product(prefix_ref, parts, i):
    total = parts[0][i]
    for part in parts[1:]:
        total += part[i].astype(jnp.float32)
    high = total.astype(jnp.bfloat16)
    low = (total - high.astype(jnp.float32)).astype(jnp.bfloat16)
    dims = (((0,), (0,)), ((), ()))
    prefix = prefix_ref[i]
    return (
        lax.dot_general(prefix, high, dims, preferred_element_type=jnp.float32)
        + lax.dot_general(prefix, low, dims, preferred_element_type=jnp.float32)
    ) * UNSCALE


def middle_kernel(prefix_ref, s0, s1, s2, s3, psi_ref, payload_ref, level_ref):
    blocks = [owner_product(prefix_ref, (s0, s1, s2, s3), i) for i in range(2)]
    squares = jnp.sum(
        blocks[0] * blocks[0] + blocks[1] * blocks[1], axis=(0, 1), keepdims=True
    )
    squares = jnp.broadcast_to(squares, (16, N))
    level = squares[0:1, :] * (1.0 / (2 * N * N)) + 1e-06
    factor = lax.rsqrt(level)
    for i in range(2):
        psi_ref[i] = blocks[i].astype(jnp.bfloat16)
        vector = (blocks[i] * factor).astype(jnp.bfloat16)
        payload_ref[i * N : i * N + N, :] = jnp.dot(
            prefix_ref[i], vector, preferred_element_type=jnp.float32
        ).astype(jnp.bfloat16)
    high = squares.astype(jnp.bfloat16).astype(jnp.float32)
    mid = (squares - high).astype(jnp.bfloat16).astype(jnp.float32)
    low = squares - high - mid
    row = lax.broadcasted_iota(jnp.int32, (16, N), 0)
    parts = jnp.where(row == 0, high, jnp.where(row == 1, mid, jnp.where(row == 2, low, 0.0)))
    payload_ref[2 * N : 2 * N + 16, :] = parts.astype(jnp.bfloat16)
    level_ref[...] = jnp.broadcast_to(level, (8, N))


def last_kernel(prefix_ref, s0, s1, s2, s3, level_ref, total_ref, out_ref):
    overall = lax.rsqrt(total_ref[0:1, :] * (1.0 / (16 * N * N)) + 1e-06)
    ratio = jnp.where(overall > 0.0, overall * jnp.sqrt(level_ref[0:1, :]), 0.0)
    for i in range(2):
        block = owner_product(prefix_ref, (s0, s1, s2, s3), i)
        out_ref[i] = (block * ratio).astype(jnp.bfloat16)


def gather_op(payload):
    mine = [payload] + [lax.ppermute(payload, "x", shift(NX, d)) for d in range(1, NX)]
    out = []
    for part in mine:
        out += [part, lax.ppermute(part, "c", shift(NC, 1))]
    return out


def scatter_sum(keep, send):
    other = lax.ppermute(send, "c", shift(NC, 1))
    block = (2, N, N)
    f32 = jax.ShapeDtypeStruct(block, jnp.float32)
    bf16 = jax.ShapeDtypeStruct(block, jnp.bfloat16)
    sums = call(add_kernel, (f32, bf16, bf16, bf16), [VMEM] * 2, [VMEM] * 4, (keep, other),
                limit=16 << 20)
    return [sums[0]] + [lax.ppermute(sums[d], "x", shift(NX, d)) for d in range(1, NX)]


def on_device(label_map, site_blocks, left_ops, right_ops, wavefunction):
    k_ops = left_ops.shape[0]
    z, y, x, c = (lax.axis_index(a) for a in ("z", "y", "x", "c"))
    at = jnp.stack([z * NY + y, x * 2 + c, y, z, x, c, z, z]).astype(jnp.int32)
    code = jax.ShapeDtypeStruct((2, CODE_ROWS, N), jnp.int16)
    pair = jax.ShapeDtypeStruct((2, N, N), jnp.bfloat16)
    half = jax.ShapeDtypeStruct((NX, 2, N, N), jnp.bfloat16)
    row = jax.ShapeDtypeStruct((8, N), jnp.float32)

    maps = lax.all_to_all(
        jnp.broadcast_to(label_map, (NZ * NY, 16)), SEG, 0, 0, tiled=True
    )
    own_code, inverse = call(
        select_kernel,
        (code, jax.ShapeDtypeStruct((16,), jnp.int32)),
        [SMEM, SMEM, VMEM],
        [VMEM, SMEM],
        (at, maps, site_blocks[0]),
        limit=16 << 20,
    )
    row_codes = [own_code] + [lax.ppermute(own_code, "y", shift(NY, d)) for d in range(1, NY)]
    total_code, before = call(
        row_kernel,
        (
            jax.ShapeDtypeStruct((NZ, 2, CODE_ROWS, N), jnp.int16),
            jax.ShapeDtypeStruct((2, N, N), jnp.float32),
        ),
        [SMEM] + [VMEM] * 4,
        [VMEM] * 2,
        (at, *row_codes),
        [pltpu.VMEM((NY, 2, N, N), jnp.float32)],
        limit=16 << 20,
    )
    codes = lax.all_to_all(total_code, "z", 0, 0, tiled=True)
    payload = call(
        chain_kernel,
        jax.ShapeDtypeStruct((4, N, N), jnp.bfloat16),
        [SMEM] + [VMEM] * 3,
        VMEM,
        (at, codes, before, wavefunction[0]),
        limit=16 << 20,
    )
    flops = 2 * k_ops * 16 * 2 * N * N * N
    limit = 24 << 20
    held = pltpu.VMEM((16, N, N), jnp.bfloat16)
    keep, send, prefix = call(
        functools.partial(apply_kernel, True, k_ops),
        (half, half, pair),
        [SMEM] * 2 + [VMEM] * 10,
        [VMEM] * 3,
        (at, inverse, left_ops, right_ops[0], *gather_op(payload)),
        [held, held],
        flops=flops,
        limit=limit,
    )
    parts = scatter_sum(keep, send)
    first_out, payload, level = call(
        middle_kernel,
        (pair, jax.ShapeDtypeStruct((2 * N + 16, N), jnp.bfloat16), row),
        [VMEM] * 5,
        [VMEM] * 3,
        (prefix, *parts),
        limit=16 << 20,
    )
    keep, send, total = call(
        functools.partial(apply_kernel, False, k_ops),
        (half, half, row),
        [SMEM] * 2 + [VMEM] * 10,
        [VMEM] * 3,
        (at, inverse, left_ops, right_ops[0], *gather_op(payload)),
        [held],
        flops=flops,
        limit=limit,
    )
    parts = scatter_sum(keep, send)
    second_out = call(
        last_kernel, pair, [VMEM] * 7, VMEM, (prefix, *parts, level, total), limit=16 << 20
    )
    return (first_out[None], second_out[None])


def solution(mesh):
    split = Mesh(mesh.devices.reshape(NZ, NY, NX, NC), ("z", "y", "x", "c"))
    placed = (
        P(SEG, None),
        P(SEG, None, None, None),
        P(OP, None, None, None),
        P(SEG, OP, None, None, None),
        P(SEG, OP, None, None),
    )
    return jax.shard_map(
        on_device,
        mesh=split,
        in_specs=placed,
        out_specs=(P(SEG, OP, None, None), P(SEG, OP, None, None)),
        check_vma=False,
    )
```

```python
import functools

import jax
import jax.numpy as jnp
from jax import lax
from jax.experimental import pallas as pl
from jax.experimental.pallas import tpu as pltpu
from jax.sharding import Mesh
from jax.sharding import PartitionSpec as P

SEG = ("z", "y")
OP = ("x", "c")
NZ, NY, NX, NC = 8, 4, 4, 2
N = 128
CODE_ROWS = N + 16
SCALE = 2.0**-27
UNSCALE = 2.0**54
VMEM = pl.BlockSpec(memory_space=pltpu.VMEM)
SMEM = pl.BlockSpec(memory_space=pltpu.SMEM)
HBM = pl.BlockSpec(memory_space=pltpu.HBM)
LN2 = 0.6931471805599453


def shift(n, d):
    return [(i, (i + d) % n) for i in range(n)]


def call(
    kernel, outs, specs, out_specs, args, scratch=(), flops=0, limit=None, moved=1 << 20
):
    return pl.pallas_call(
        kernel,
        out_shape=outs,
        in_specs=specs,
        out_specs=out_specs,
        scratch_shapes=list(scratch),
        cost_estimate=pl.CostEstimate(flops=flops, bytes_accessed=moved, transcendentals=0),
        compiler_params=pltpu.CompilerParams(vmem_limit_bytes=limit),
    )(*args)


def encode(x):
    top = jnp.maximum(jnp.max(jnp.abs(x), axis=0, keepdims=True), 1e-30)
    power = jnp.ceil(jnp.log(top) * (1.0 / LN2))
    coded = jnp.round(x * (jnp.exp(power * -LN2) * 32760.0)).astype(jnp.int32)
    powers = jnp.broadcast_to(power, (16, N)).astype(jnp.int32)
    return coded.astype(jnp.int16), powers.astype(jnp.int16)


def decode(ref):
    coded = ref[0:N, :].astype(jnp.int32).astype(jnp.float32)
    power = ref[N:CODE_ROWS, :].astype(jnp.int32).astype(jnp.float32)[0:1, :]
    return coded * (jnp.exp(power * LN2) * (1.0 / 32760.0))


def split(x):
    high = x.astype(jnp.bfloat16)
    return high, (x - high.astype(jnp.float32)).astype(jnp.bfloat16)


def mm(a, b):
    (a1, a2), (b1, b2) = split(a), split(b)
    dot = functools.partial(jnp.dot, preferred_element_type=jnp.float32)
    return dot(a1, b1) + (dot(a1, b2) + dot(a2, b1))


def code_kernel(blocks_ref, codes_ref):
    for q in range(16):
        coded, powers = encode(blocks_ref[q])
        codes_ref[q, 0:N, :] = coded
        codes_ref[q, N:CODE_ROWS, :] = powers


def select_kernel(at_ref, maps_ref, codes_ref, after_ref, code_ref, inverse_ref):
    seg = at_ref[0]
    own = at_ref[1]

    def step(s, labels):
        return tuple(maps_ref[s, label] for label in labels)

    labels = lax.fori_loop(0, seg, step, tuple(jnp.int32(q) for q in range(16)))
    for q in range(16):
        inverse_ref[labels[q]] = jnp.int32(q)
    for i in range(2):
        label = jnp.int32(0)
        for q in range(16):
            label = jnp.where(own * 2 + i == q, labels[q], label)
        code_ref[i] = codes_ref[label]


def fetch_kernel(pieces, after_ref, source_ref, target_ref, done_ref, sems):
    size = source_ref.shape[0] // pieces
    copies = [
        pltpu.make_async_copy(
            source_ref.at[pl.ds(j * size, size)], target_ref.at[pl.ds(j * size, size)], sems.at[j]
        )
        for j in range(pieces)
    ]
    for copy in copies:
        copy.start()
    for copy in copies:
        copy.wait()
    done_ref[0] = after_ref[0]


def fetch(source, after, pieces, limit):
    return call(
        functools.partial(fetch_kernel, pieces),
        (
            jax.ShapeDtypeStruct(source.shape, source.dtype),
            jax.ShapeDtypeStruct((8,), jnp.int32),
        ),
        [SMEM, HBM],
        [VMEM, SMEM],
        (after, source),
        [pltpu.SemaphoreType.DMA((pieces,))],
        moved=12 << 20,
        limit=limit << 20,
    )


def row_kernel(at_ref, s0, s1, s2, s3, after_ref, code_ref, before_ref, held):
    y = at_ref[2]
    for d, ref in enumerate((s0, s1, s2, s3)):
        for i in range(2):
            held[lax.rem(y - d + NY, NY), i] = decode(ref.at[i])
    diagonal = lax.broadcasted_iota(jnp.int32, (N, N), 0) == lax.broadcasted_iota(
        jnp.int32, (N, N), 1
    )
    identity = diagonal.astype(jnp.float32)
    for i in range(2):
        first = mm(held[0, i], held[1, i])
        last = mm(held[2, i], held[3, i])
        three = mm(first, held[2, i])
        coded, powers = encode(mm(first, last))
        for z in range(NZ):
            code_ref[z, i, 0:N, :] = coded
            code_ref[z, i, N:CODE_ROWS, :] = powers
        low = jnp.where(y == 0, identity, held[0, i])
        high = jnp.where(y == 2, first, three)
        before_ref[i] = jnp.where(y < 2, low, high)


def chain_kernel(at_ref, codes_ref, before_ref, psi_ref, out_ref):
    z = at_ref[3]
    diagonal = lax.broadcasted_iota(jnp.int32, (N, N), 0) == lax.broadcasted_iota(
        jnp.int32, (N, N), 1
    )
    identity = diagonal.astype(jnp.float32)
    for i in range(2):
        factors = [
            jnp.where(k < z, decode(codes_ref.at[k, i]), identity) for k in range(NZ - 1)
        ] + [before_ref[i]]
        while len(factors) > 1:
            factors = [mm(factors[j], factors[j + 1]) for j in range(0, len(factors), 2)]
        out_ref[i] = (factors[0] * SCALE).astype(jnp.bfloat16)
        out_ref[2 + i] = psi_ref[i]


def sources(at_ref):
    own, x, c = at_ref[1], at_ref[4], at_ref[5]
    return [
        lax.rem(x - d + NX, NX) * 2 + (c if same == 0 else 1 - c)
        for d in range(NX)
        for same in range(2)
    ]


def sector_products(keep, at_ref, inverse_ref, left_ref, right_ref, phi_of, out_ref):
    x, c = at_ref[4], at_ref[5]
    core = c if keep else 1 - c
    k_ops = left_ref.shape[0]
    for d in range(NX):
        source = 2 * ((NX - d) % NX) + (0 if keep else 1)
        for i in range(2):
            p = (lax.rem(x + d, NX) * 2 + core) * 2 + i
            q = inverse_ref[p]
            left = left_ref[:, q].reshape(k_ops * N, N)
            rows = jnp.dot(left, phi_of(source, i, q), preferred_element_type=jnp.float32)
            rows = rows.astype(jnp.bfloat16)
            half = jnp.concatenate([rows[k * N : k * N + N] for k in range(k_ops)], axis=1)
            right = jnp.concatenate([right_ref[k, p] for k in range(k_ops)], axis=1)
            out_ref[d, i] = lax.dot_general(
                half, right, (((1,), (1,)), ((), ())), preferred_element_type=jnp.float32
            ).astype(jnp.bfloat16)


def first_kernel(keep, at_ref, inverse_ref, left_ref, right_ref, *refs):
    parts, out_ref, prefixes = refs[:8], refs[8], refs[-1]
    x, c = at_ref[4], at_ref[5]
    for source, part in zip(sources(at_ref), parts):
        for i in range(2):
            prefixes[source * 2 + i] = part[i]
    if keep:
        for i in range(2):
            refs[9][i] = prefixes[inverse_ref[(x * 2 + c) * 2 + i]]

    def phi_of(source, i, q):
        return jnp.dot(
            prefixes[q], parts[source][2 + i], preferred_element_type=jnp.float32
        ).astype(jnp.bfloat16)

    sector_products(keep, at_ref, inverse_ref, left_ref, right_ref, phi_of, out_ref)


def second_kernel(keep, at_ref, inverse_ref, left_ref, right_ref, *refs):
    parts, out_ref = refs[:8], refs[8]
    if keep:
        total = jnp.zeros((1, N), jnp.float32)
        for part in parts:
            level = part[2 * N : 2 * N + 16, :].astype(jnp.float32)
            total += jnp.sum(level, axis=0, keepdims=True)
        refs[9][...] = jnp.broadcast_to(total, (8, N))

    def phi_of(source, i, q):
        return parts[source][i * N : i * N + N, :]

    sector_products(keep, at_ref, inverse_ref, left_ref, right_ref, phi_of, out_ref)


def add_kernel(keep_ref, other_ref, s0, s1, s2, s3):
    for d, ref in enumerate((s0, s1, s2, s3)):
        both = keep_ref[d].astype(jnp.float32) + other_ref[d].astype(jnp.float32)
        ref[...] = both.astype(ref.dtype)


def owner_product(prefix_ref, parts, i):
    total = parts[0][i]
    for part in parts[1:]:
        total += part[i].astype(jnp.float32)
    high = total.astype(jnp.bfloat16)
    low = (total - high.astype(jnp.float32)).astype(jnp.bfloat16)
    dims = (((0,), (0,)), ((), ()))
    prefix = prefix_ref[i]
    return (
        lax.dot_general(prefix, high, dims, preferred_element_type=jnp.float32)
        + lax.dot_general(prefix, low, dims, preferred_element_type=jnp.float32)
    ) * UNSCALE


def middle_kernel(prefix_ref, s0, s1, s2, s3, psi_ref, payload_ref, level_ref):
    blocks = [owner_product(prefix_ref, (s0, s1, s2, s3), i) for i in range(2)]
    squares = jnp.sum(
        blocks[0] * blocks[0] + blocks[1] * blocks[1], axis=(0, 1), keepdims=True
    )
    squares = jnp.broadcast_to(squares, (16, N))
    level = squares[0:1, :] * (1.0 / (2 * N * N)) + 1e-06
    factor = lax.rsqrt(level)
    for i in range(2):
        psi_ref[i] = blocks[i].astype(jnp.bfloat16)
        vector = (blocks[i] * factor).astype(jnp.bfloat16)
        payload_ref[i * N : i * N + N, :] = jnp.dot(
            prefix_ref[i], vector, preferred_element_type=jnp.float32
        ).astype(jnp.bfloat16)
    high = squares.astype(jnp.bfloat16).astype(jnp.float32)
    mid = (squares - high).astype(jnp.bfloat16).astype(jnp.float32)
    low = squares - high - mid
    row = lax.broadcasted_iota(jnp.int32, (16, N), 0)
    parts = jnp.where(row == 0, high, jnp.where(row == 1, mid, jnp.where(row == 2, low, 0.0)))
    payload_ref[2 * N : 2 * N + 16, :] = parts.astype(jnp.bfloat16)
    level_ref[...] = jnp.broadcast_to(level, (8, N))


def last_kernel(prefix_ref, s0, s1, s2, s3, level_ref, total_ref, out_ref):
    overall = lax.rsqrt(total_ref[0:1, :] * (1.0 / (16 * N * N)) + 1e-06)
    ratio = jnp.where(overall > 0.0, overall * jnp.sqrt(level_ref[0:1, :]), 0.0)
    for i in range(2):
        block = owner_product(prefix_ref, (s0, s1, s2, s3), i)
        out_ref[i] = (block * ratio).astype(jnp.bfloat16)


def gather_op(payload):
    mine = [payload] + [lax.ppermute(payload, "x", shift(NX, d)) for d in range(1, NX)]
    out = []
    for part in mine:
        out += [part, lax.ppermute(part, "c", shift(NC, 1))]
    return out


def scatter_sum(keep, other):
    block = (2, N, N)
    f32 = jax.ShapeDtypeStruct(block, jnp.float32)
    bf16 = jax.ShapeDtypeStruct(block, jnp.bfloat16)
    sums = call(add_kernel, (f32, bf16, bf16, bf16), [VMEM] * 2, [VMEM] * 4, (keep, other),
                limit=16 << 20)
    return [sums[0]] + [lax.ppermute(sums[d], "x", shift(NX, d)) for d in range(1, NX)]


def on_device(label_map, site_blocks, left_ops, right_ops, wavefunction):
    k_ops = left_ops.shape[0]
    z, y, x, c = (lax.axis_index(a) for a in ("z", "y", "x", "c"))
    at = jnp.stack([z * NY + y, x * 2 + c, y, z, x, c, z, z]).astype(jnp.int32)
    code = jax.ShapeDtypeStruct((2, CODE_ROWS, N), jnp.int16)
    pair = jax.ShapeDtypeStruct((2, N, N), jnp.bfloat16)
    half = jax.ShapeDtypeStruct((NX, 2, N, N), jnp.bfloat16)
    row = jax.ShapeDtypeStruct((8, N), jnp.float32)

    maps = lax.all_to_all(
        jnp.broadcast_to(label_map, (NZ * NY, 16)), SEG, 0, 0, tiled=True
    )
    blocks_code = call(
        code_kernel,
        jax.ShapeDtypeStruct((16, CODE_ROWS, N), jnp.int16),
        [VMEM],
        VMEM,
        (site_blocks[0],),
        limit=16 << 20,
    )
    left, fetched = fetch(left_ops, at, 1, 48)
    own_code, inverse = call(
        select_kernel,
        (code, jax.ShapeDtypeStruct((16,), jnp.int32)),
        [SMEM, SMEM, VMEM, SMEM],
        [VMEM, SMEM],
        (at, maps, blocks_code, fetched),
        limit=16 << 20,
    )
    row_codes = [own_code] + [lax.ppermute(own_code, "y", shift(NY, d)) for d in range(1, NY)]
    right, fetched = fetch(right_ops[0], inverse, 1, 44)
    total_code, before = call(
        row_kernel,
        (
            jax.ShapeDtypeStruct((NZ, 2, CODE_ROWS, N), jnp.int16),
            jax.ShapeDtypeStruct((2, N, N), jnp.float32),
        ),
        [SMEM] + [VMEM] * 4 + [SMEM],
        [VMEM] * 2,
        (at, *row_codes, fetched),
        [pltpu.VMEM((NY, 2, N, N), jnp.float32)],
        limit=16 << 20,
    )
    codes = lax.all_to_all(total_code, "z", 0, 0, tiled=True)
    payload = call(
        chain_kernel,
        jax.ShapeDtypeStruct((4, N, N), jnp.bfloat16),
        [SMEM] + [VMEM] * 3,
        VMEM,
        (at, codes, before, wavefunction[0]),
        limit=16 << 20,
    )
    held = pltpu.VMEM((16, N, N), jnp.bfloat16)
    def apply(kernel, extra, scratch, args):
        run = functools.partial(
            call,
            specs=[SMEM] * 2 + [VMEM] * (2 + len(args)),
            args=(at, inverse, left, right, *args),
            scratch=scratch,
            flops=2 * k_ops * 8 * 2 * N * N * N,
            limit=20 << 20,
        )
        send = run(functools.partial(kernel, False), half, out_specs=VMEM)
        other = lax.ppermute(send, "c", shift(NC, 1))
        keep, more = run(functools.partial(kernel, True), (half, extra), out_specs=[VMEM] * 2)
        return scatter_sum(keep, other), more

    parts, prefix = apply(first_kernel, pair, [held], gather_op(payload))
    first_out, payload, level = call(
        middle_kernel,
        (pair, jax.ShapeDtypeStruct((2 * N + 16, N), jnp.bfloat16), row),
        [VMEM] * 5,
        [VMEM] * 3,
        (prefix, *parts),
        limit=16 << 20,
    )
    parts, total = apply(second_kernel, row, [], gather_op(payload))
    second_out = call(
        last_kernel, pair, [VMEM] * 7, VMEM, (prefix, *parts, level, total), limit=16 << 20
    )
    return (first_out[None], second_out[None])


def solution(mesh):
    split = Mesh(mesh.devices.reshape(NZ, NY, NX, NC), ("z", "y", "x", "c"))
    placed = (
        P(SEG, None),
        P(SEG, None, None, None),
        P(OP, None, None, None),
        P(SEG, OP, None, None, None),
        P(SEG, OP, None, None),
    )
    return jax.shard_map(
        on_device,
        mesh=split,
        in_specs=placed,
        out_specs=(P(SEG, OP, None, None), P(SEG, OP, None, None)),
        check_vma=False,
    )
```

```python
import functools

import jax
import jax.numpy as jnp
from jax import lax
from jax.experimental import pallas as pl
from jax.experimental.pallas import tpu as pltpu
from jax.sharding import Mesh
from jax.sharding import PartitionSpec as P

SEG = ("z", "y")
OP = ("x", "c")
NZ, NY, NX, NC = 8, 4, 4, 2
N = 128
CODE_ROWS = N + 16
SCALE = 2.0**-27
UNSCALE = 2.0**54
VMEM = pl.BlockSpec(memory_space=pltpu.VMEM)
SMEM = pl.BlockSpec(memory_space=pltpu.SMEM)
HBM = pl.BlockSpec(memory_space=pltpu.HBM)
LN2 = 0.6931471805599453


def shift(n, d):
    return [(i, (i + d) % n) for i in range(n)]


def call(
    kernel, outs, specs, out_specs, args, scratch=(), flops=0, limit=None, moved=1 << 20
):
    return pl.pallas_call(
        kernel,
        out_shape=outs,
        in_specs=specs,
        out_specs=out_specs,
        scratch_shapes=list(scratch),
        cost_estimate=pl.CostEstimate(flops=flops, bytes_accessed=moved, transcendentals=0),
        compiler_params=pltpu.CompilerParams(vmem_limit_bytes=limit),
    )(*args)


def place(name):
    return lax.axis_index(name)


def encode(x):
    top = jnp.maximum(jnp.max(jnp.abs(x), axis=0, keepdims=True), 1e-30)
    power = jnp.ceil(jnp.log(top) * (1.0 / LN2))
    coded = jnp.round(x * (jnp.exp(power * -LN2) * 32760.0)).astype(jnp.int32)
    powers = jnp.broadcast_to(power, (16, N)).astype(jnp.int32)
    return coded.astype(jnp.int16), powers.astype(jnp.int16)


def decode(ref):
    coded = ref[0:N, :].astype(jnp.int32).astype(jnp.float32)
    power = ref[N:CODE_ROWS, :].astype(jnp.int32).astype(jnp.float32)[0:1, :]
    return coded * (jnp.exp(power * LN2) * (1.0 / 32760.0))


def split(x):
    high = x.astype(jnp.bfloat16)
    return high, (x - high.astype(jnp.float32)).astype(jnp.bfloat16)


def mm(a, b):
    (a1, a2), (b1, b2) = split(a), split(b)
    dot = functools.partial(jnp.dot, preferred_element_type=jnp.float32)
    return dot(a1, b1) + (dot(a1, b2) + dot(a2, b1))


def code_kernel(blocks_ref, codes_ref):
    for q in range(16):
        coded, powers = encode(blocks_ref[q])
        codes_ref[q, 0:N, :] = coded
        codes_ref[q, N:CODE_ROWS, :] = powers


def select_kernel(maps_ref, codes_ref, code_ref, inverse_ref):
    seg = place("z") * NY + place("y")
    own = place("x") * 2 + place("c")

    def step(s, labels):
        return tuple(maps_ref[s, label] for label in labels)

    labels = lax.fori_loop(0, seg, step, tuple(jnp.int32(q) for q in range(16)))
    for q in range(16):
        inverse_ref[labels[q]] = jnp.int32(q)
    for i in range(2):
        label = jnp.int32(0)
        for q in range(16):
            label = jnp.where(own * 2 + i == q, labels[q], label)
        code_ref[i] = codes_ref[label]


def fetch_kernel(after_ref, left_hbm, right_hbm, left_ref, right_ref, sems):
    copies = [
        pltpu.make_async_copy(left_hbm, left_ref, sems.at[0]),
        pltpu.make_async_copy(right_hbm, right_ref, sems.at[1]),
    ]
    for copy in copies:
        copy.start()
    for copy in copies:
        copy.wait()


def row_kernel(s0, s1, s2, s3, after_ref, code_ref, before_ref, held):
    y = place("y")
    for d, ref in enumerate((s0, s1, s2, s3)):
        for i in range(2):
            held[lax.rem(y - d + NY, NY), i] = decode(ref.at[i])
    diagonal = lax.broadcasted_iota(jnp.int32, (N, N), 0) == lax.broadcasted_iota(
        jnp.int32, (N, N), 1
    )
    identity = diagonal.astype(jnp.float32)
    for i in range(2):
        first = mm(held[0, i], held[1, i])
        last = mm(held[2, i], held[3, i])
        three = mm(first, held[2, i])
        coded, powers = encode(mm(first, last))
        for z in range(NZ):
            code_ref[z, i, 0:N, :] = coded
            code_ref[z, i, N:CODE_ROWS, :] = powers
        low = jnp.where(y == 0, identity, held[0, i])
        high = jnp.where(y == 2, first, three)
        before_ref[i] = jnp.where(y < 2, low, high)


def chain_kernel(codes_ref, before_ref, psi_ref, out_ref):
    z = place("z")
    diagonal = lax.broadcasted_iota(jnp.int32, (N, N), 0) == lax.broadcasted_iota(
        jnp.int32, (N, N), 1
    )
    identity = diagonal.astype(jnp.float32)
    for i in range(2):
        factors = [
            jnp.where(k < z, decode(codes_ref.at[k, i]), identity) for k in range(NZ - 1)
        ] + [before_ref[i]]
        while len(factors) > 1:
            factors = [mm(factors[j], factors[j + 1]) for j in range(0, len(factors), 2)]
        out_ref[i] = (factors[0] * SCALE).astype(jnp.bfloat16)
        out_ref[2 + i] = psi_ref[i]


def sources():
    x, c = place("x"), place("c")
    return [
        lax.rem(x - d + NX, NX) * 2 + (c if same == 0 else 1 - c)
        for d in range(NX)
        for same in range(2)
    ]


def sector_products(keep, inverse_ref, left_ref, right_ref, phi_of, out_ref):
    x, c = place("x"), place("c")
    core = c if keep else 1 - c
    k_ops = left_ref.shape[0]
    for d in range(NX):
        source = 2 * ((NX - d) % NX) + (0 if keep else 1)
        for i in range(2):
            p = (lax.rem(x + d, NX) * 2 + core) * 2 + i
            q = inverse_ref[p]
            left = left_ref[:, q].reshape(k_ops * N, N)
            rows = jnp.dot(left, phi_of(source, i, q), preferred_element_type=jnp.float32)
            rows = rows.astype(jnp.bfloat16)
            half = jnp.concatenate([rows[k * N : k * N + N] for k in range(k_ops)], axis=1)
            right = jnp.concatenate([right_ref[k, p] for k in range(k_ops)], axis=1)
            out_ref[d, i] = lax.dot_general(
                half, right, (((1,), (1,)), ((), ())), preferred_element_type=jnp.float32
            ).astype(jnp.bfloat16)


def first_kernel(keep, inverse_ref, left_ref, right_ref, *refs):
    parts, out_ref, prefixes = refs[:8], refs[8], refs[-1]
    x, c = place("x"), place("c")
    for source, part in zip(sources(), parts):
        for i in range(2):
            prefixes[source * 2 + i] = part[i]
    if keep:
        for i in range(2):
            refs[9][i] = prefixes[inverse_ref[(x * 2 + c) * 2 + i]]

    def phi_of(source, i, q):
        return jnp.dot(
            prefixes[q], parts[source][2 + i], preferred_element_type=jnp.float32
        ).astype(jnp.bfloat16)

    sector_products(keep, inverse_ref, left_ref, right_ref, phi_of, out_ref)


def second_kernel(keep, inverse_ref, left_ref, right_ref, *refs):
    parts, out_ref = refs[:8], refs[8]
    if keep:
        total = jnp.zeros((1, N), jnp.float32)
        for part in parts:
            level = part[2 * N : 2 * N + 16, :].astype(jnp.float32)
            total += jnp.sum(level, axis=0, keepdims=True)
        refs[9][...] = jnp.broadcast_to(total, (8, N))

    def phi_of(source, i, q):
        return parts[source][i * N : i * N + N, :]

    sector_products(keep, inverse_ref, left_ref, right_ref, phi_of, out_ref)


def add_kernel(keep_ref, other_ref, s0, s1, s2, s3):
    for d, ref in enumerate((s0, s1, s2, s3)):
        both = keep_ref[d].astype(jnp.float32) + other_ref[d].astype(jnp.float32)
        ref[...] = both.astype(ref.dtype)


def owner_product(prefix_ref, parts, i):
    total = parts[0][i]
    for part in parts[1:]:
        total += part[i].astype(jnp.float32)
    high = total.astype(jnp.bfloat16)
    low = (total - high.astype(jnp.float32)).astype(jnp.bfloat16)
    dims = (((0,), (0,)), ((), ()))
    prefix = prefix_ref[i]
    return (
        lax.dot_general(prefix, high, dims, preferred_element_type=jnp.float32)
        + lax.dot_general(prefix, low, dims, preferred_element_type=jnp.float32)
    ) * UNSCALE


def middle_kernel(prefix_ref, s0, s1, s2, s3, psi_ref, payload_ref, level_ref):
    blocks = [owner_product(prefix_ref, (s0, s1, s2, s3), i) for i in range(2)]
    squares = jnp.sum(
        blocks[0] * blocks[0] + blocks[1] * blocks[1], axis=(0, 1), keepdims=True
    )
    squares = jnp.broadcast_to(squares, (16, N))
    level = squares[0:1, :] * (1.0 / (2 * N * N)) + 1e-06
    factor = lax.rsqrt(level)
    for i in range(2):
        psi_ref[i] = blocks[i].astype(jnp.bfloat16)
        vector = (blocks[i] * factor).astype(jnp.bfloat16)
        payload_ref[i * N : i * N + N, :] = jnp.dot(
            prefix_ref[i], vector, preferred_element_type=jnp.float32
        ).astype(jnp.bfloat16)
    high = squares.astype(jnp.bfloat16).astype(jnp.float32)
    mid = (squares - high).astype(jnp.bfloat16).astype(jnp.float32)
    low = squares - high - mid
    row = lax.broadcasted_iota(jnp.int32, (16, N), 0)
    parts = jnp.where(row == 0, high, jnp.where(row == 1, mid, jnp.where(row == 2, low, 0.0)))
    payload_ref[2 * N : 2 * N + 16, :] = parts.astype(jnp.bfloat16)
    level_ref[...] = jnp.broadcast_to(level, (8, N))


def last_kernel(prefix_ref, s0, s1, s2, s3, level_ref, total_ref, out_ref):
    overall = lax.rsqrt(total_ref[0:1, :] * (1.0 / (16 * N * N)) + 1e-06)
    ratio = jnp.where(overall > 0.0, overall * jnp.sqrt(level_ref[0:1, :]), 0.0)
    for i in range(2):
        block = owner_product(prefix_ref, (s0, s1, s2, s3), i)
        out_ref[i] = (block * ratio).astype(jnp.bfloat16)


def gather_op(payload):
    mine = [payload] + [lax.ppermute(payload, "x", shift(NX, d)) for d in range(1, NX)]
    out = []
    for part in mine:
        out += [part, lax.ppermute(part, "c", shift(NC, 1))]
    return out


def scatter_sum(keep, other):
    block = (2, N, N)
    f32 = jax.ShapeDtypeStruct(block, jnp.float32)
    bf16 = jax.ShapeDtypeStruct(block, jnp.bfloat16)
    sums = call(add_kernel, (f32, bf16, bf16, bf16), [VMEM] * 2, [VMEM] * 4, (keep, other),
                limit=16 << 20)
    return [sums[0]] + [lax.ppermute(sums[d], "x", shift(NX, d)) for d in range(1, NX)]


def on_device(label_map, site_blocks, left_ops, right_ops, wavefunction):
    k_ops = left_ops.shape[0]
    code = jax.ShapeDtypeStruct((2, CODE_ROWS, N), jnp.int16)
    pair = jax.ShapeDtypeStruct((2, N, N), jnp.bfloat16)
    half = jax.ShapeDtypeStruct((NX, 2, N, N), jnp.bfloat16)
    row = jax.ShapeDtypeStruct((8, N), jnp.float32)

    maps = lax.all_to_all(
        jnp.broadcast_to(label_map, (NZ * NY, 16)), SEG, 0, 0, tiled=True
    )
    blocks_code = call(
        code_kernel,
        jax.ShapeDtypeStruct((16, CODE_ROWS, N), jnp.int16),
        [VMEM],
        VMEM,
        (site_blocks[0],),
        limit=16 << 20,
    )
    own_code, inverse = call(
        select_kernel,
        (code, jax.ShapeDtypeStruct((16,), jnp.int32)),
        [SMEM, VMEM],
        [VMEM, SMEM],
        (maps, blocks_code),
        limit=16 << 20,
    )
    row_codes = [own_code] + [lax.ppermute(own_code, "y", shift(NY, d)) for d in range(1, NY)]
    left, right = call(
        fetch_kernel,
        (
            jax.ShapeDtypeStruct(left_ops.shape, jnp.bfloat16),
            jax.ShapeDtypeStruct(right_ops.shape[1:], jnp.bfloat16),
        ),
        [VMEM, HBM, HBM],
        [VMEM] * 2,
        (own_code, left_ops, right_ops[0]),
        [pltpu.SemaphoreType.DMA((2,))],
        moved=25 << 20,
        limit=38 << 20,
    )
    total_code, before = call(
        row_kernel,
        (
            jax.ShapeDtypeStruct((NZ, 2, CODE_ROWS, N), jnp.int16),
            jax.ShapeDtypeStruct((2, N, N), jnp.float32),
        ),
        [VMEM] * 5,
        [VMEM] * 2,
        (*row_codes, right),
        [pltpu.VMEM((NY, 2, N, N), jnp.float32)],
        limit=16 << 20,
    )
    codes = lax.all_to_all(total_code, "z", 0, 0, tiled=True)
    payload = call(
        chain_kernel,
        jax.ShapeDtypeStruct((4, N, N), jnp.bfloat16),
        [VMEM] * 3,
        VMEM,
        (codes, before, wavefunction[0]),
        limit=16 << 20,
    )
    held = pltpu.VMEM((16, N, N), jnp.bfloat16)
    def apply(kernel, extra, scratch, args):
        run = functools.partial(
            call,
            specs=[SMEM] + [VMEM] * (2 + len(args)),
            args=(inverse, left, right, *args),
            scratch=scratch,
            flops=2 * k_ops * 8 * 2 * N * N * N,
            limit=20 << 20,
        )
        send = run(functools.partial(kernel, False), half, out_specs=VMEM)
        other = lax.ppermute(send, "c", shift(NC, 1))
        keep, more = run(functools.partial(kernel, True), (half, extra), out_specs=[VMEM] * 2)
        return scatter_sum(keep, other), more

    parts, prefix = apply(first_kernel, pair, [held], gather_op(payload))
    first_out, payload, level = call(
        middle_kernel,
        (pair, jax.ShapeDtypeStruct((2 * N + 16, N), jnp.bfloat16), row),
        [VMEM] * 5,
        [VMEM] * 3,
        (prefix, *parts),
        limit=16 << 20,
    )
    parts, total = apply(second_kernel, row, [], gather_op(payload))
    second_out = call(
        last_kernel, pair, [VMEM] * 7, VMEM, (prefix, *parts, level, total), limit=16 << 20
    )
    return (first_out[None], second_out[None])


def solution(mesh):
    split = Mesh(mesh.devices.reshape(NZ, NY, NX, NC), ("z", "y", "x", "c"))
    placed = (
        P(SEG, None),
        P(SEG, None, None, None),
        P(OP, None, None, None),
        P(SEG, OP, None, None, None),
        P(SEG, OP, None, None),
    )
    return jax.shard_map(
        on_device,
        mesh=split,
        in_specs=placed,
        out_specs=(P(SEG, OP, None, None), P(SEG, OP, None, None)),
        check_vma=False,
    )
```

```python
import functools

import jax
import jax.numpy as jnp
from jax import lax
from jax.experimental import pallas as pl
from jax.experimental.pallas import tpu as pltpu
from jax.sharding import Mesh
from jax.sharding import PartitionSpec as P

SEG = ("z", "y")
OP = ("x", "c")
NZ, NY, NX, NC = 8, 4, 4, 2
N = 128
CODE_ROWS = N + 16
SCALE = 2.0**-27
UNSCALE = 2.0**54
VMEM = pl.BlockSpec(memory_space=pltpu.VMEM)
SMEM = pl.BlockSpec(memory_space=pltpu.SMEM)
HBM = pl.BlockSpec(memory_space=pltpu.HBM)
LN2 = 0.6931471805599453


def shift(n, d):
    return [(i, (i + d) % n) for i in range(n)]


def call(
    kernel, outs, specs, out_specs, args, scratch=(), flops=0, limit=None, moved=1 << 20
):
    return pl.pallas_call(
        kernel,
        out_shape=outs,
        in_specs=specs,
        out_specs=out_specs,
        scratch_shapes=list(scratch),
        cost_estimate=pl.CostEstimate(flops=flops, bytes_accessed=moved, transcendentals=0),
        compiler_params=pltpu.CompilerParams(vmem_limit_bytes=limit),
    )(*args)


def place(name):
    return lax.axis_index(name)


def encode(x):
    top = jnp.maximum(jnp.max(jnp.abs(x), axis=0, keepdims=True), 1e-30)
    power = jnp.ceil(jnp.log(top) * (1.0 / LN2))
    coded = jnp.round(x * (jnp.exp(power * -LN2) * 32760.0)).astype(jnp.int32)
    powers = jnp.broadcast_to(power, (16, N)).astype(jnp.int32)
    return coded.astype(jnp.int16), powers.astype(jnp.int16)


def decode(ref):
    coded = ref[0:N, :].astype(jnp.int32).astype(jnp.float32)
    power = ref[N:CODE_ROWS, :].astype(jnp.int32).astype(jnp.float32)[0:1, :]
    return coded * (jnp.exp(power * LN2) * (1.0 / 32760.0))


def split(x):
    high = x.astype(jnp.bfloat16)
    return high, (x - high.astype(jnp.float32)).astype(jnp.bfloat16)


def mm(a, b):
    (a1, a2), (b1, b2) = split(a), split(b)
    dot = functools.partial(jnp.dot, preferred_element_type=jnp.float32)
    return dot(a1, b1) + (dot(a1, b2) + dot(a2, b1))


def code_kernel(blocks_ref, codes_ref):
    for q in range(16):
        coded, powers = encode(blocks_ref[q])
        codes_ref[q, 0:N, :] = coded
        codes_ref[q, N:CODE_ROWS, :] = powers


def select_kernel(maps_ref, codes_ref, code_ref, inverse_ref):
    seg = place("z") * NY + place("y")
    own = place("x") * 2 + place("c")

    def step(s, labels):
        return tuple(maps_ref[s, label] for label in labels)

    labels = lax.fori_loop(0, seg, step, tuple(jnp.int32(q) for q in range(16)))
    for q in range(16):
        inverse_ref[labels[q]] = jnp.int32(q)
    for i in range(2):
        label = jnp.int32(0)
        for q in range(16):
            label = jnp.where(own * 2 + i == q, labels[q], label)
        code_ref[i] = codes_ref[label]


def fetch_kernel(after_ref, left_hbm, right_hbm, left_ref, right_ref, sems):
    copies = [
        pltpu.make_async_copy(left_hbm, left_ref, sems.at[0]),
        pltpu.make_async_copy(right_hbm, right_ref, sems.at[1]),
    ]
    for copy in copies:
        copy.start()
    for copy in copies:
        copy.wait()


def row_kernel(s0, s1, s2, s3, after_ref, code_ref, before_ref, held):
    y = place("y")
    for d, ref in enumerate((s0, s1, s2, s3)):
        for i in range(2):
            held[lax.rem(y - d + NY, NY), i] = decode(ref.at[i])
    diagonal = lax.broadcasted_iota(jnp.int32, (N, N), 0) == lax.broadcasted_iota(
        jnp.int32, (N, N), 1
    )
    identity = diagonal.astype(jnp.float32)
    for i in range(2):
        first = mm(held[0, i], held[1, i])
        last = mm(held[2, i], held[3, i])
        three = mm(first, held[2, i])
        coded, powers = encode(mm(first, last))
        for z in range(NZ):
            code_ref[z, i, 0:N, :] = coded
            code_ref[z, i, N:CODE_ROWS, :] = powers
        low = jnp.where(y == 0, identity, held[0, i])
        high = jnp.where(y == 2, first, three)
        before_ref[i] = jnp.where(y < 2, low, high)


def chain_kernel(codes_ref, before_ref, psi_ref, out_ref):
    z = place("z")
    diagonal = lax.broadcasted_iota(jnp.int32, (N, N), 0) == lax.broadcasted_iota(
        jnp.int32, (N, N), 1
    )
    identity = diagonal.astype(jnp.float32)
    for i in range(2):
        factors = [
            jnp.where(k < z, decode(codes_ref.at[k, i]), identity) for k in range(NZ - 1)
        ] + [before_ref[i]]
        while len(factors) > 1:
            factors = [mm(factors[j], factors[j + 1]) for j in range(0, len(factors), 2)]
        out_ref[i] = (factors[0] * SCALE).astype(jnp.bfloat16)
        out_ref[2 + i] = psi_ref[i]


def sources():
    x, c = place("x"), place("c")
    return [
        lax.rem(x - d + NX, NX) * 2 + (c if same == 0 else 1 - c)
        for d in range(NX)
        for same in range(2)
    ]


def sector_products(same, ds, inverse_ref, left_ref, right_ref, phi_of, out_ref):
    x, c = place("x"), place("c")
    core = c if same else 1 - c
    k_ops = left_ref.shape[0]
    for j, d in enumerate(ds):
        source = 2 * ((NX - d) % NX) + (0 if same else 1)
        for i in range(2):
            p = (lax.rem(x + d, NX) * 2 + core) * 2 + i
            q = inverse_ref[p]
            left = left_ref[:, q].reshape(k_ops * N, N)
            rows = jnp.dot(left, phi_of(source, i, q), preferred_element_type=jnp.float32)
            rows = rows.astype(jnp.bfloat16)
            half = jnp.concatenate([rows[k * N : k * N + N] for k in range(k_ops)], axis=1)
            right = jnp.concatenate([right_ref[k, p] for k in range(k_ops)], axis=1)
            out_ref[j, i] = lax.dot_general(
                half, right, (((1,), (1,)), ((), ())), preferred_element_type=jnp.float32
            ).astype(jnp.bfloat16)


def first_kernel(same, ds, inverse_ref, left_ref, right_ref, *refs):
    parts = refs[:8]
    if same:
        prefixes, out_ref = refs[8], refs[9]
    else:
        out_ref, prefixes = refs[8], refs[9]
        for source, part in zip(sources(), parts):
            for i in range(2):
                prefixes[source * 2 + i] = part[i]
    if len(refs) > 10:
        own = place("x") * 2 + place("c")
        for i in range(2):
            refs[10][i] = prefixes[inverse_ref[own * 2 + i]]

    def phi_of(source, i, q):
        return jnp.dot(
            prefixes[q], parts[source][2 + i], preferred_element_type=jnp.float32
        ).astype(jnp.bfloat16)

    sector_products(same, ds, inverse_ref, left_ref, right_ref, phi_of, out_ref)


def second_kernel(same, ds, inverse_ref, left_ref, right_ref, *refs):
    parts, out_ref = refs[:8], refs[8]
    if len(refs) > 9:
        total = jnp.zeros((1, N), jnp.float32)
        for part in parts:
            level = part[2 * N : 2 * N + 16, :].astype(jnp.float32)
            total += jnp.sum(level, axis=0, keepdims=True)
        refs[9][...] = jnp.broadcast_to(total, (8, N))

    def phi_of(source, i, q):
        return parts[source][i * N : i * N + N, :]

    sector_products(same, ds, inverse_ref, left_ref, right_ref, phi_of, out_ref)


def add_kernel(far_ref, other_ref, s1, s2, s3):
    for d, ref in enumerate((s1, s2, s3)):
        both = far_ref[d].astype(jnp.float32) + other_ref[d + 1].astype(jnp.float32)
        ref[...] = both.astype(ref.dtype)


def owner_product(prefix_ref, parts, i):
    near, other, *moved = parts
    total = near[0, i].astype(jnp.float32) + other[0, i].astype(jnp.float32)
    for part in moved:
        total += part[i].astype(jnp.float32)
    high = total.astype(jnp.bfloat16)
    low = (total - high.astype(jnp.float32)).astype(jnp.bfloat16)
    dims = (((0,), (0,)), ((), ()))
    prefix = prefix_ref[i]
    return (
        lax.dot_general(prefix, high, dims, preferred_element_type=jnp.float32)
        + lax.dot_general(prefix, low, dims, preferred_element_type=jnp.float32)
    ) * UNSCALE


def middle_kernel(prefix_ref, near, other, s1, s2, s3, psi_ref, payload_ref, level_ref):
    blocks = [owner_product(prefix_ref, (near, other, s1, s2, s3), i) for i in range(2)]
    squares = jnp.sum(
        blocks[0] * blocks[0] + blocks[1] * blocks[1], axis=(0, 1), keepdims=True
    )
    squares = jnp.broadcast_to(squares, (16, N))
    level = squares[0:1, :] * (1.0 / (2 * N * N)) + 1e-06
    factor = lax.rsqrt(level)
    for i in range(2):
        psi_ref[i] = blocks[i].astype(jnp.bfloat16)
        vector = (blocks[i] * factor).astype(jnp.bfloat16)
        payload_ref[i * N : i * N + N, :] = jnp.dot(
            prefix_ref[i], vector, preferred_element_type=jnp.float32
        ).astype(jnp.bfloat16)
    high = squares.astype(jnp.bfloat16).astype(jnp.float32)
    mid = (squares - high).astype(jnp.bfloat16).astype(jnp.float32)
    low = squares - high - mid
    row = lax.broadcasted_iota(jnp.int32, (16, N), 0)
    parts = jnp.where(row == 0, high, jnp.where(row == 1, mid, jnp.where(row == 2, low, 0.0)))
    payload_ref[2 * N : 2 * N + 16, :] = parts.astype(jnp.bfloat16)
    level_ref[...] = jnp.broadcast_to(level, (8, N))


def last_kernel(prefix_ref, near, other, s1, s2, s3, level_ref, total_ref, out_ref):
    overall = lax.rsqrt(total_ref[0:1, :] * (1.0 / (16 * N * N)) + 1e-06)
    ratio = jnp.where(overall > 0.0, overall * jnp.sqrt(level_ref[0:1, :]), 0.0)
    for i in range(2):
        block = owner_product(prefix_ref, (near, other, s1, s2, s3), i)
        out_ref[i] = (block * ratio).astype(jnp.bfloat16)


def gather_op(payload):
    mine = [payload] + [lax.ppermute(payload, "x", shift(NX, d)) for d in range(1, NX)]
    out = []
    for part in mine:
        out += [part, lax.ppermute(part, "c", shift(NC, 1))]
    return out


def on_device(label_map, site_blocks, left_ops, right_ops, wavefunction):
    k_ops = left_ops.shape[0]
    code = jax.ShapeDtypeStruct((2, CODE_ROWS, N), jnp.int16)
    pair = jax.ShapeDtypeStruct((2, N, N), jnp.bfloat16)
    half = jax.ShapeDtypeStruct((NX, 2, N, N), jnp.bfloat16)
    row = jax.ShapeDtypeStruct((8, N), jnp.float32)

    maps = lax.all_to_all(
        jnp.broadcast_to(label_map, (NZ * NY, 16)), SEG, 0, 0, tiled=True
    )
    blocks_code = call(
        code_kernel,
        jax.ShapeDtypeStruct((16, CODE_ROWS, N), jnp.int16),
        [VMEM],
        VMEM,
        (site_blocks[0],),
        limit=16 << 20,
    )
    own_code, inverse = call(
        select_kernel,
        (code, jax.ShapeDtypeStruct((16,), jnp.int32)),
        [SMEM, VMEM],
        [VMEM, SMEM],
        (maps, blocks_code),
        limit=16 << 20,
    )
    row_codes = [own_code] + [lax.ppermute(own_code, "y", shift(NY, d)) for d in range(1, NY)]
    left, right = call(
        fetch_kernel,
        (
            jax.ShapeDtypeStruct(left_ops.shape, jnp.bfloat16),
            jax.ShapeDtypeStruct(right_ops.shape[1:], jnp.bfloat16),
        ),
        [VMEM, HBM, HBM],
        [VMEM] * 2,
        (own_code, left_ops, right_ops[0]),
        [pltpu.SemaphoreType.DMA((2,))],
        moved=25 << 20,
        limit=38 << 20,
    )
    total_code, before = call(
        row_kernel,
        (
            jax.ShapeDtypeStruct((NZ, 2, CODE_ROWS, N), jnp.int16),
            jax.ShapeDtypeStruct((2, N, N), jnp.float32),
        ),
        [VMEM] * 5,
        [VMEM] * 2,
        (*row_codes, right),
        [pltpu.VMEM((NY, 2, N, N), jnp.float32)],
        limit=16 << 20,
    )
    codes = lax.all_to_all(total_code, "z", 0, 0, tiled=True)
    payload = call(
        chain_kernel,
        jax.ShapeDtypeStruct((4, N, N), jnp.bfloat16),
        [VMEM] * 3,
        VMEM,
        (codes, before, wavefunction[0]),
        limit=16 << 20,
    )
    array = lambda *lengths: jax.ShapeDtypeStruct((*lengths, N, N), jnp.bfloat16)

    def apply(kernel, shared, extra, args):
        def run(same, ds, out, args):
            several = isinstance(out, tuple)
            return call(
                functools.partial(kernel, same, ds),
                out,
                [SMEM] + [VMEM] * (2 + len(args)),
                [VMEM] * len(out) if several else VMEM,
                (inverse, left, right, *args),
                flops=2 * k_ops * 2 * len(ds) * 2 * N * N * N,
                limit=20 << 20,
            )

        if shared is None:
            send = run(False, (0, 1, 2, 3), half, args)
        else:
            send, more = run(False, (0, 1, 2, 3), (half, shared), args)
            args = (*args, more)
        other = lax.ppermute(send, "c", shift(NC, 1))
        far = run(True, (1, 2, 3), array(3, 2), args)
        sums = call(
            add_kernel, (pair,) * 3, [VMEM] * 2, [VMEM] * 3, (far, other), limit=16 << 20
        )
        moved = [lax.ppermute(sums[d - 1], "x", shift(NX, d)) for d in range(1, NX)]
        near, extra = run(True, (0,), (array(1, 2), extra), args)
        return [near, other, *moved], extra

    parts, prefix = apply(first_kernel, array(16), pair, gather_op(payload))
    first_out, payload, level = call(
        middle_kernel,
        (pair, jax.ShapeDtypeStruct((2 * N + 16, N), jnp.bfloat16), row),
        [VMEM] * 6,
        [VMEM] * 3,
        (prefix, *parts),
        limit=16 << 20,
    )
    parts, total = apply(second_kernel, None, row, gather_op(payload))
    second_out = call(
        last_kernel, pair, [VMEM] * 8, VMEM, (prefix, *parts, level, total), limit=16 << 20
    )
    return (first_out[None], second_out[None])


def solution(mesh):
    split = Mesh(mesh.devices.reshape(NZ, NY, NX, NC), ("z", "y", "x", "c"))
    placed = (
        P(SEG, None),
        P(SEG, None, None, None),
        P(OP, None, None, None),
        P(SEG, OP, None, None, None),
        P(SEG, OP, None, None),
    )
    return jax.shard_map(
        on_device,
        mesh=split,
        in_specs=placed,
        out_specs=(P(SEG, OP, None, None), P(SEG, OP, None, None)),
        check_vma=False,
    )
```

```python
import functools

import jax
import jax.numpy as jnp
from jax import lax
from jax.experimental import pallas as pl
from jax.experimental.pallas import tpu as pltpu
from jax.sharding import Mesh
from jax.sharding import PartitionSpec as P

SEG = ("z", "y")
OP = ("x", "c")
NZ, NY, NX, NC = 8, 4, 4, 2
N = 128
CODE_ROWS = N + 16
SCALE = 2.0**-27
UNSCALE = 2.0**54
VMEM = pl.BlockSpec(memory_space=pltpu.VMEM)
SMEM = pl.BlockSpec(memory_space=pltpu.SMEM)
HBM = pl.BlockSpec(memory_space=pltpu.HBM)
LN2 = 0.6931471805599453


def shift(n, d):
    return [(i, (i + d) % n) for i in range(n)]


def call(
    kernel, outs, specs, out_specs, args, scratch=(), flops=0, limit=None, moved=1 << 20
):
    return pl.pallas_call(
        kernel,
        out_shape=outs,
        in_specs=specs,
        out_specs=out_specs,
        scratch_shapes=list(scratch),
        cost_estimate=pl.CostEstimate(flops=flops, bytes_accessed=moved, transcendentals=0),
        compiler_params=pltpu.CompilerParams(vmem_limit_bytes=limit),
    )(*args)


def place(name):
    return lax.axis_index(name)


def encode(x):
    top = jnp.maximum(jnp.max(jnp.abs(x), axis=0, keepdims=True), 1e-30)
    power = jnp.ceil(jnp.log(top) * (1.0 / LN2))
    coded = jnp.round(x * (jnp.exp(power * -LN2) * 32760.0)).astype(jnp.int32)
    powers = jnp.broadcast_to(power, (16, N)).astype(jnp.int32)
    return coded.astype(jnp.int16), powers.astype(jnp.int16)


def decode(ref):
    coded = ref[0:N, :].astype(jnp.int32).astype(jnp.float32)
    power = ref[N:CODE_ROWS, :].astype(jnp.int32).astype(jnp.float32)[0:1, :]
    return coded * (jnp.exp(power * LN2) * (1.0 / 32760.0))


def split(x):
    high = x.astype(jnp.bfloat16)
    return high, (x - high.astype(jnp.float32)).astype(jnp.bfloat16)


def mm(a, b):
    (a1, a2), (b1, b2) = split(a), split(b)
    dot = functools.partial(jnp.dot, preferred_element_type=jnp.float32)
    return dot(a1, b1) + (dot(a1, b2) + dot(a2, b1))


def code_kernel(blocks_ref, codes_ref):
    for q in range(16):
        coded, powers = encode(blocks_ref[q])
        codes_ref[q, 0:N, :] = coded
        codes_ref[q, N:CODE_ROWS, :] = powers


def follow(maps_ref, labels):
    seg = place("z") * NY + place("y")

    def step(s, labels):
        return tuple(maps_ref[s, label] for label in labels)

    return lax.fori_loop(0, seg, step, tuple(labels))


def select_kernel(maps_ref, codes_ref, code_ref):
    own = (place("x") * 2 + place("c")) * 2
    for i, label in enumerate(follow(maps_ref, (own, own + 1))):
        code_ref[i] = codes_ref[label]


def fetch_kernel(
    after_ref, maps_ref, left_hbm, right_hbm, left_ref, right_ref, inverse_ref, maps, inverse, sems
):
    copies = [
        pltpu.make_async_copy(left_hbm, left_ref, sems.at[0]),
        pltpu.make_async_copy(right_hbm, right_ref, sems.at[1]),
    ]
    tables = pltpu.make_async_copy(maps_ref, maps, sems.at[2])
    for copy in [tables] + copies:
        copy.start()
    tables.wait()
    for q, label in enumerate(follow(maps, [jnp.int32(q) for q in range(16)])):
        inverse[label] = jnp.int32(q)
    result = pltpu.make_async_copy(inverse, inverse_ref, sems.at[3])
    result.start()
    for copy in [result] + copies:
        copy.wait()


def row_kernel(s0, s1, s2, s3, after_ref, code_ref, before_ref, held):
    y = place("y")
    for d, ref in enumerate((s0, s1, s2, s3)):
        for i in range(2):
            held[lax.rem(y - d + NY, NY), i] = decode(ref.at[i])
    diagonal = lax.broadcasted_iota(jnp.int32, (N, N), 0) == lax.broadcasted_iota(
        jnp.int32, (N, N), 1
    )
    identity = diagonal.astype(jnp.float32)
    for i in range(2):
        first = mm(held[0, i], held[1, i])
        last = mm(held[2, i], held[3, i])
        three = mm(first, held[2, i])
        coded, powers = encode(mm(first, last))
        for z in range(NZ):
            code_ref[z, i, 0:N, :] = coded
            code_ref[z, i, N:CODE_ROWS, :] = powers
        low = jnp.where(y == 0, identity, held[0, i])
        high = jnp.where(y == 2, first, three)
        before_ref[i] = jnp.where(y < 2, low, high)


def chain_kernel(codes_ref, before_ref, psi_ref, out_ref):
    z = place("z")
    diagonal = lax.broadcasted_iota(jnp.int32, (N, N), 0) == lax.broadcasted_iota(
        jnp.int32, (N, N), 1
    )
    identity = diagonal.astype(jnp.float32)
    for i in range(2):
        factors = [
            jnp.where(k < z, decode(codes_ref.at[k, i]), identity) for k in range(NZ - 1)
        ] + [before_ref[i]]
        while len(factors) > 1:
            factors = [mm(factors[j], factors[j + 1]) for j in range(0, len(factors), 2)]
        out_ref[i] = (factors[0] * SCALE).astype(jnp.bfloat16)
        out_ref[2 + i] = psi_ref[i]


def sources():
    x, c = place("x"), place("c")
    return [
        lax.rem(x - d + NX, NX) * 2 + (c if same == 0 else 1 - c)
        for d in range(NX)
        for same in range(2)
    ]


def sector_products(same, ds, inverse_ref, left_ref, right_ref, phi_of, out_ref):
    x, c = place("x"), place("c")
    core = c if same else 1 - c
    k_ops = left_ref.shape[0]
    for j, d in enumerate(ds):
        source = 2 * ((NX - d) % NX) + (0 if same else 1)
        for i in range(2):
            p = (lax.rem(x + d, NX) * 2 + core) * 2 + i
            q = inverse_ref[p]
            left = left_ref[:, q].reshape(k_ops * N, N)
            rows = jnp.dot(left, phi_of(source, i, q), preferred_element_type=jnp.float32)
            rows = rows.astype(jnp.bfloat16)
            half = jnp.concatenate([rows[k * N : k * N + N] for k in range(k_ops)], axis=1)
            right = jnp.concatenate([right_ref[k, p] for k in range(k_ops)], axis=1)
            out_ref[j, i] = lax.dot_general(
                half, right, (((1,), (1,)), ((), ())), preferred_element_type=jnp.float32
            ).astype(jnp.bfloat16)


def first_kernel(same, ds, inverse_ref, left_ref, right_ref, *refs):
    parts = refs[:8]
    if same:
        prefixes, out_ref = refs[8], refs[9]
    else:
        out_ref, prefixes = refs[8], refs[9]
        for source, part in zip(sources(), parts):
            for i in range(2):
                prefixes[source * 2 + i] = part[i]
    if len(refs) > 10:
        own = place("x") * 2 + place("c")
        for i in range(2):
            refs[10][i] = prefixes[inverse_ref[own * 2 + i]]

    def phi_of(source, i, q):
        return jnp.dot(
            prefixes[q], parts[source][2 + i], preferred_element_type=jnp.float32
        ).astype(jnp.bfloat16)

    sector_products(same, ds, inverse_ref, left_ref, right_ref, phi_of, out_ref)


def second_kernel(same, ds, inverse_ref, left_ref, right_ref, *refs):
    parts, out_ref = refs[:8], refs[8]
    if len(refs) > 9:
        total = jnp.zeros((1, N), jnp.float32)
        for part in parts:
            level = part[2 * N : 2 * N + 16, :].astype(jnp.float32)
            total += jnp.sum(level, axis=0, keepdims=True)
        refs[9][...] = jnp.broadcast_to(total, (8, N))

    def phi_of(source, i, q):
        return parts[source][i * N : i * N + N, :]

    sector_products(same, ds, inverse_ref, left_ref, right_ref, phi_of, out_ref)


def add_kernel(far_ref, other_ref, s1, s2, s3):
    for d, ref in enumerate((s1, s2, s3)):
        both = far_ref[d].astype(jnp.float32) + other_ref[d + 1].astype(jnp.float32)
        ref[...] = both.astype(ref.dtype)


def owner_product(prefix_ref, parts, i):
    near, other, *moved = parts
    total = near[0, i].astype(jnp.float32) + other[0, i].astype(jnp.float32)
    for part in moved:
        total += part[i].astype(jnp.float32)
    high = total.astype(jnp.bfloat16)
    low = (total - high.astype(jnp.float32)).astype(jnp.bfloat16)
    dims = (((0,), (0,)), ((), ()))
    prefix = prefix_ref[i]
    return (
        lax.dot_general(prefix, high, dims, preferred_element_type=jnp.float32)
        + lax.dot_general(prefix, low, dims, preferred_element_type=jnp.float32)
    ) * UNSCALE


def middle_kernel(prefix_ref, near, other, s1, s2, s3, psi_ref, payload_ref, level_ref):
    blocks = [owner_product(prefix_ref, (near, other, s1, s2, s3), i) for i in range(2)]
    squares = jnp.sum(
        blocks[0] * blocks[0] + blocks[1] * blocks[1], axis=(0, 1), keepdims=True
    )
    squares = jnp.broadcast_to(squares, (16, N))
    level = squares[0:1, :] * (1.0 / (2 * N * N)) + 1e-06
    factor = lax.rsqrt(level)
    for i in range(2):
        psi_ref[i] = blocks[i].astype(jnp.bfloat16)
        vector = (blocks[i] * factor).astype(jnp.bfloat16)
        payload_ref[i * N : i * N + N, :] = jnp.dot(
            prefix_ref[i], vector, preferred_element_type=jnp.float32
        ).astype(jnp.bfloat16)
    high = squares.astype(jnp.bfloat16).astype(jnp.float32)
    mid = (squares - high).astype(jnp.bfloat16).astype(jnp.float32)
    low = squares - high - mid
    row = lax.broadcasted_iota(jnp.int32, (16, N), 0)
    parts = jnp.where(row == 0, high, jnp.where(row == 1, mid, jnp.where(row == 2, low, 0.0)))
    payload_ref[2 * N : 2 * N + 16, :] = parts.astype(jnp.bfloat16)
    level_ref[...] = jnp.broadcast_to(level, (8, N))


def last_kernel(prefix_ref, near, other, s1, s2, s3, level_ref, total_ref, out_ref):
    overall = lax.rsqrt(total_ref[0:1, :] * (1.0 / (16 * N * N)) + 1e-06)
    ratio = jnp.where(overall > 0.0, overall * jnp.sqrt(level_ref[0:1, :]), 0.0)
    for i in range(2):
        block = owner_product(prefix_ref, (near, other, s1, s2, s3), i)
        out_ref[i] = (block * ratio).astype(jnp.bfloat16)


def gather_op(payload):
    mine = [payload] + [lax.ppermute(payload, "x", shift(NX, d)) for d in range(1, NX)]
    out = []
    for part in mine:
        out += [part, lax.ppermute(part, "c", shift(NC, 1))]
    return out


def on_device(label_map, site_blocks, left_ops, right_ops, wavefunction):
    k_ops = left_ops.shape[0]
    code = jax.ShapeDtypeStruct((2, CODE_ROWS, N), jnp.int16)
    pair = jax.ShapeDtypeStruct((2, N, N), jnp.bfloat16)
    half = jax.ShapeDtypeStruct((NX, 2, N, N), jnp.bfloat16)
    row = jax.ShapeDtypeStruct((8, N), jnp.float32)

    maps = lax.all_to_all(
        jnp.broadcast_to(label_map, (NZ * NY, 16)), SEG, 0, 0, tiled=True
    )
    blocks_code = call(
        code_kernel,
        jax.ShapeDtypeStruct((16, CODE_ROWS, N), jnp.int16),
        [VMEM],
        VMEM,
        (site_blocks[0],),
        limit=16 << 20,
    )
    own_code = call(
        select_kernel,
        code,
        [SMEM, VMEM],
        VMEM,
        (maps, blocks_code),
        limit=16 << 20,
    )
    row_codes = [own_code] + [lax.ppermute(own_code, "y", shift(NY, d)) for d in range(1, NY)]
    left, right, inverse = call(
        fetch_kernel,
        (
            jax.ShapeDtypeStruct(left_ops.shape, jnp.bfloat16),
            jax.ShapeDtypeStruct(right_ops.shape[1:], jnp.bfloat16),
            jax.ShapeDtypeStruct((16,), jnp.int32),
        ),
        [VMEM, VMEM, HBM, HBM],
        [VMEM] * 3,
        (own_code, maps, left_ops, right_ops[0]),
        [
            pltpu.SMEM((NZ * NY, 16), jnp.int32),
            pltpu.SMEM((16,), jnp.int32),
            pltpu.SemaphoreType.DMA((4,)),
        ],
        moved=25 << 20,
        limit=38 << 20,
    )
    total_code, before = call(
        row_kernel,
        (
            jax.ShapeDtypeStruct((NZ, 2, CODE_ROWS, N), jnp.int16),
            jax.ShapeDtypeStruct((2, N, N), jnp.float32),
        ),
        [VMEM] * 5,
        [VMEM] * 2,
        (*row_codes, right),
        [pltpu.VMEM((NY, 2, N, N), jnp.float32)],
        limit=16 << 20,
    )
    codes = lax.all_to_all(total_code, "z", 0, 0, tiled=True)
    payload = call(
        chain_kernel,
        jax.ShapeDtypeStruct((4, N, N), jnp.bfloat16),
        [VMEM] * 3,
        VMEM,
        (codes, before, wavefunction[0]),
        limit=16 << 20,
    )
    array = lambda *lengths: jax.ShapeDtypeStruct((*lengths, N, N), jnp.bfloat16)

    def apply(kernel, shared, extra, args):
        def run(same, ds, out, args):
            several = isinstance(out, tuple)
            return call(
                functools.partial(kernel, same, ds),
                out,
                [SMEM] + [VMEM] * (2 + len(args)),
                [VMEM] * len(out) if several else VMEM,
                (inverse, left, right, *args),
                flops=2 * k_ops * 2 * len(ds) * 2 * N * N * N,
                limit=20 << 20,
            )

        if shared is None:
            send = run(False, (0, 1, 2, 3), half, args)
        else:
            send, more = run(False, (0, 1, 2, 3), (half, shared), args)
            args = (*args, more)
        other = lax.ppermute(send, "c", shift(NC, 1))
        far = run(True, (1, 2, 3), array(3, 2), args)
        sums = call(
            add_kernel, (pair,) * 3, [VMEM] * 2, [VMEM] * 3, (far, other), limit=16 << 20
        )
        moved = [lax.ppermute(sums[d - 1], "x", shift(NX, d)) for d in range(1, NX)]
        near, extra = run(True, (0,), (array(1, 2), extra), args)
        return [near, other, *moved], extra

    parts, prefix = apply(first_kernel, array(16), pair, gather_op(payload))
    first_out, payload, level = call(
        middle_kernel,
        (pair, jax.ShapeDtypeStruct((2 * N + 16, N), jnp.bfloat16), row),
        [VMEM] * 6,
        [VMEM] * 3,
        (prefix, *parts),
        limit=16 << 20,
    )
    parts, total = apply(second_kernel, None, row, gather_op(payload))
    second_out = call(
        last_kernel, pair, [VMEM] * 8, VMEM, (prefix, *parts, level, total), limit=16 << 20
    )
    return (first_out[None], second_out[None])


def solution(mesh):
    split = Mesh(mesh.devices.reshape(NZ, NY, NX, NC), ("z", "y", "x", "c"))
    placed = (
        P(SEG, None),
        P(SEG, None, None, None),
        P(OP, None, None, None),
        P(SEG, OP, None, None, None),
        P(SEG, OP, None, None),
    )
    return jax.shard_map(
        on_device,
        mesh=split,
        in_specs=placed,
        out_specs=(P(SEG, OP, None, None), P(SEG, OP, None, None)),
        check_vma=False,
    )
```
